32 devices in a mesh: leaf: 32 (over z, y, x, core).
Axes of the slice: x: 2, y: 2, z: 4, core: 2. Of those that a mesh axis runs over, the one named last changes fastest.
Arguments:
- points: bfloat16 [49152, 128], P('leaf'), may hold values from -20 to 20
- weights: bfloat16 [49152, 256], P('leaf'), may hold values from -4 to 4
- targets: bfloat16 [49152, 256], P('leaf'), may hold values from -4 to 4
- near_mask: int32 [32, 4], P('leaf'), may hold values from 0 to 1, as said below
- leaf_skeleton: int32 [32, 256], P('leaf'), may hold values from 0 to 1535, as said below
- node_skeleton: int32 [4, 32, 256], P(None, 'leaf'), may hold values from 0 to 511, as said below
Outputs:
- updated: bfloat16 [49152, 256], P('leaf')
- residual: float32 [49152, 256], P('leaf')
The draws below stay inside these ranges and needn't reach their ends.
Inputs may be any that keep to these rules, and one draw needn't show every extreme that they name: near_mask is 0 where the listed leaf would lie outside the tree; leaf i lists leaf j exactly when leaf j lists leaf i; the number of listed leaves differs from leaf to leaf. `leaf_skeleton`: row i holds 256 distinct increasing point numbers counted within leaf i. `node_skeleton`: entry [l, i] holds 256 distinct increasing positions in the union of the two children's skeletons of the level l + 1 node containing leaf i; equal for all leaves of that node.
All inputs are finite; a program needn't handle non-finite values.
Results may differ from the reference program's by a relative error of at most 0.0034.
Values may be sent and summed in bfloat16 or wider, within the bound.
A program may use at most 64 MiB of HBM per device.

```python
import math
import jax
import jax.numpy as jnp
from jax import lax

F = 128
R = 256
S = 256
PTS_DEV = 1536
LEVELS = 5
REACH = 2
LEAVES = 32
NPTS = 49152


def draw_points(key, part):
    latent_dims = max(F // 16, 4)
    bound = float(F // 8 + 4)
    spread = (0.2 * F) ** 0.5
    radius = (0.75 * F) ** 0.5
    noise_scale = 0.5 ** 0.5
    column = jnp.arange(F, dtype=jnp.int32)[None, :]
    leaf_pos = (jnp.arange(NPTS, dtype=jnp.int32) // PTS_DEV).astype(jnp.float32)[:, None]
    angle = 2.0 * math.pi * leaf_pos / 64.0
    helix = jnp.where(column == latent_dims, radius * jnp.cos(angle), 0.0)
    helix = helix + jnp.where(column == latent_dims + 1, radius * jnp.sin(angle), 0.0)
    key_base = jax.random.fold_in(key, 5)
    base = jnp.clip(jax.random.normal(key_base, (NPTS, F), jnp.float32), -6.0, 6.0)
    latent_scale = spread * jnp.ones((NPTS, 1), jnp.float32)
    scale = jnp.where(column < latent_dims, latent_scale, noise_scale)
    values = jnp.clip(helix + scale * base, -bound, bound)
    return values.astype(jnp.bfloat16)


def draw_near_mask(key, part):
    bits = jax.random.randint(jax.random.fold_in(key, 11), (LEAVES, REACH), 0, 2).astype(jnp.int32)
    leaf_ids = jnp.arange(LEAVES, dtype=jnp.int32)[:, None]
    offsets = jnp.arange(1, REACH + 1, dtype=jnp.int32)[None, :]
    ahead = jnp.where(leaf_ids + offsets < LEAVES, bits, 0)
    source_rows = jnp.clip(leaf_ids - offsets, 0, LEAVES - 1)
    source_cols = jnp.broadcast_to(offsets - 1, (LEAVES, REACH))
    behind = jnp.where(leaf_ids - offsets >= 0, ahead[source_rows, source_cols], 0)
    return jnp.concatenate([ahead, behind], axis=1).astype(jnp.int32)


def draw_leaf_skeleton(key, part):
    keys = jax.random.split(jax.random.fold_in(key, 23), LEAVES)

    def choose(single):
        return jnp.sort(jax.random.permutation(single, PTS_DEV)[:S])
    return jax.vmap(choose)(keys).astype(jnp.int32)


def draw_node_skeleton(key, part):
    base = jax.random.fold_in(key, 37)
    leaf_ids = jnp.arange(LEAVES, dtype=jnp.int32)
    level_ids = jnp.arange(LEVELS - 1, dtype=jnp.int32)

    def per_level(tree_level):

        def per_leaf(index):
            single = jax.random.fold_in(jax.random.fold_in(base, tree_level), jnp.right_shift(index, tree_level + 1))
            return jnp.sort(jax.random.permutation(single, 2 * S)[:S])
        return jax.vmap(per_leaf)(leaf_ids)
    return jax.vmap(per_level)(level_ids).astype(jnp.int32)


def steps_of(key, extent, shards, least, largest):
    loudness, own = 1.0, jax.random.fold_in(key, 6)
    for dim, shards_of in shards:
        draws = jnp.exp(jax.random.uniform(jax.random.fold_in(own, dim), (shards_of,), jnp.float32, least / len(shards), largest / len(shards)))
        loudness = loudness * jnp.repeat(draws, extent[dim] // shards_of).reshape([-1 if axis == dim else 1 for axis in range(len(extent))])
    return loudness


def normal_values(stream_key, dims, scale, reach, shards=(), held_as=jnp.bfloat16):
    drawn = jax.random.normal(stream_key, dims, jnp.float32) * scale
    if len(shards) > 0:
        drawn = steps_of(stream_key, dims, shards, -0.22, 0.18) * drawn
    return jnp.clip(drawn, min=-reach, max=reach).astype(held_as)


def setup_inputs(seed: int = 0) -> dict:
    streams_of = jax.random.split(jax.random.key(seed), 7)
    return {
        "points": draw_points(jax.random.fold_in(streams_of[6], 71), 0),
        "weights": normal_values(streams_of[1], (NPTS, R), 1.0, 4.0, ((0, 32),)),
        "targets": normal_values(streams_of[2], (NPTS, R), 1.0, 4.0, ((0, 32),)),
        "near_mask": draw_near_mask(jax.random.fold_in(streams_of[6], 71), 0),
        "leaf_skeleton": draw_leaf_skeleton(jax.random.fold_in(streams_of[6], 71), 0),
        "node_skeleton": draw_node_skeleton(jax.random.fold_in(streams_of[6], 71), 0),
    }


ridge_weight = 1.0
damping = 0.25


def kernel(left_rows, right_rows):
    left_sq = jnp.sum(jnp.square(left_rows.astype(jnp.float32)), axis=1)
    right_sq = jnp.sum(jnp.square(right_rows.astype(jnp.float32)), axis=1)
    products = lax.dot_general(left_rows, right_rows, (((1,), (1,)), ((), ())), preferred_element_type=jnp.float32)
    return jnp.exp(-(left_sq[:, None] + right_sq[None, :] - 2.0 * products) / left_rows.shape[1])


def apply_tile(own_points, remote_points, remote_weights):
    return jnp.dot(kernel(own_points, remote_points).astype(jnp.bfloat16), remote_weights, preferred_element_type=jnp.float32)


def reference(points, weights, targets, near_mask, leaf_skeleton, node_skeleton):
    leaf_points = points.reshape(LEAVES, PTS_DEV, F)
    leaf_weights = weights.reshape(LEAVES, PTS_DEV, R)
    nothing = jnp.zeros((PTS_DEV, R), jnp.float32)

    def leaf_near(index):
        own = leaf_points[index]
        total = apply_tile(own, own, leaf_weights[index])
        for offset in range(1, REACH + 1):
            for column, other in ((offset - 1, index + offset), (REACH + offset - 1, index - offset)):
                listed = near_mask[index, column] > 0
                clipped = jnp.clip(other, 0, LEAVES - 1).astype(jnp.int32)
                total = total + lax.cond(listed, lambda c: apply_tile(own, leaf_points[c], leaf_weights[c]), lambda c: nothing, clipped)
        return total

    near_field = lax.map(leaf_near, jnp.arange(LEAVES, dtype=jnp.int32))

    def leaf_charges(args):
        own, own_w, pick = args
        skel_points = jnp.take(own, pick, axis=0)
        charges = jnp.dot(kernel(skel_points, own).astype(jnp.bfloat16), own_w, preferred_element_type=jnp.float32).astype(jnp.bfloat16)
        return skel_points, charges

    skel_points, charges = lax.map(leaf_charges, (leaf_points, leaf_weights, leaf_skeleton))
    far_field = jnp.zeros((LEAVES, PTS_DEV, R), jnp.float32)
    leaf_ids = jnp.arange(LEAVES, dtype=jnp.int32)
    for tree_level in range(LEVELS):
        partner = jnp.bitwise_xor(leaf_ids, 1 << tree_level)
        partner_points = skel_points[partner]
        partner_charges = charges[partner]

        def far_terms(args):
            own, remote_points, remote_charges = args
            return jnp.dot(kernel(own, remote_points).astype(jnp.bfloat16), remote_charges, preferred_element_type=jnp.float32)

        far_field = far_field + lax.map(far_terms, (leaf_points, partner_points, partner_charges))
        if tree_level + 1 < LEVELS:
            is_upper = (jnp.right_shift(leaf_ids, tree_level) & 1) == 1
            upper_mask = is_upper[:, None, None]
            union_points = jnp.concatenate([jnp.where(upper_mask, partner_points, skel_points), jnp.where(upper_mask, skel_points, partner_points)], axis=1)
            union_charges = jnp.concatenate([jnp.where(upper_mask, partner_charges, charges), jnp.where(upper_mask, charges, partner_charges)], axis=1)

            def climb(args):
                union_p, union_c, chosen = args
                node_points = jnp.take(union_p, chosen, axis=0)
                affinity = kernel(node_points, union_p)
                transfer_share = (affinity / jnp.sum(affinity, axis=0, keepdims=True)).astype(jnp.bfloat16)
                node_charges = jnp.dot(transfer_share, union_c, preferred_element_type=jnp.float32).astype(jnp.bfloat16)
                return node_points, node_charges

            skel_points, charges = lax.map(climb, (union_points, union_charges, node_skeleton[tree_level]))
    near_flat = near_field.reshape(NPTS, R)
    far_flat = far_field.reshape(NPTS, R)
    residual = targets.astype(jnp.float32) - ridge_weight * weights.astype(jnp.float32) - near_flat - far_flat
    updated = (weights.astype(jnp.float32) + damping * residual / (1.0 + ridge_weight)).astype(jnp.bfloat16)
    return updated, residual
```

```python
import functools

import jax
import jax.numpy as jnp
from jax import lax
from jax.experimental import pallas as pl
from jax.experimental.pallas import tpu as pltpu
from jax.sharding import PartitionSpec as P

LEVELS = 5

ridge_weight = 1.0
damping = 0.25
LOG2E = 1.4426950408889634

CHUNKS = 12
BLOCKS = 6
AHEAD = 3

def pieces(rows):
    wide = rows.astype(jnp.float32)
    sq = jnp.sum(wide * wide, axis=1, keepdims=True)
    hi = sq.astype(jnp.bfloat16).astype(jnp.float32)
    rest = sq - hi
    mid = rest.astype(jnp.bfloat16).astype(jnp.float32)
    return hi, mid, rest - mid


def extra(rows, parts, first, second):
    hi, mid, low = parts
    lane = lax.broadcasted_iota(jnp.int32, rows.shape, 1)

    def picked(which, start):
        if which is None:
            return jnp.where((lane >= start) & (lane < start + 3), 1.0, 0.0)
        zero = jnp.zeros(rows.shape, jnp.float32)
        out = jnp.where(lane == start, hi, zero)
        out = jnp.where(lane == start + 1, mid, out)
        return jnp.where(lane == start + 2, low, out)

    return picked(first, 0) + picked(second, 3)


def left_form(rows, parts):
    tail = -extra(rows, parts, "norms", None)
    return jnp.concatenate(
        [(rows.astype(jnp.float32) * 2.0).astype(jnp.bfloat16), tail.astype(jnp.bfloat16)], axis=1
    )


def right_form(rows, parts):
    tail = extra(rows, parts, None, "norms")
    return jnp.concatenate([rows, tail.astype(jnp.bfloat16)], axis=1)


def affinity(left, right, features):
    s = lax.dot_general(left, right, (((1,), (1,)), ((), ())), preferred_element_type=jnp.float32)
    return jnp.exp2(s * (LOG2E / features))


def dot(a, b):
    return jnp.dot(a, b, preferred_element_type=jnp.float32)


def step(
    n,
    mask_hbm,
    points_hbm,
    weights_hbm,
    leaf_index_hbm,
    node_index_hbm,
    total,
    mask,
    points,
    weights,
    leaf_index,
    node_index,
    near_x,
    near_w,
    sib_x,
    sib_w,
    q_x,
    q_w,
    union_x,
    union_q,
    share,
    own_left,
    own_right,
    other_right,
    far_right,
    far_w,
    indices,
    load_sem,
    x_send,
    x_recv,
    r_send,
    r_recv,
    q_send,
    q_recv,
    s_send,
    s_recv,
    l_send,
    l_recv,
    f_send,
    f_recv,
):
    me = lax.axis_index("leaf")
    rows, features = points.shape
    skel = leaf_index.shape[1]
    chunk = rows // CHUNKS
    block = rows // BLOCKS
    core = lax.rem(me, 2)
    side = lax.rem(me // 2, 2)
    flip = core + side - 2 * core * side
    relay_to = me + 4 - 8 * side
    relay_from = me - 4 + 8 * side
    gives = (relay_to >= 0) & (relay_to < n)
    takes = (relay_from >= 0) & (relay_from < n)
    takes_q = (flip == 1) | takes

    def bit(level):
        return lax.rem(me // (2**level), 2)

    def across(level):
        return me + (1 - 2 * bit(level)) * (2**level)

    def greet(device):
        pl.semaphore_signal(barrier, inc=1, device_id=(device,), device_id_type=pl.DeviceIdType.MESH)

    def start(copies):
        for copy in copies:
            copy.start()

    def landed(copies):
        for copy in copies:
            copy.wait_recv()

    def left_behind(copies):
        for copy in copies:
            copy.wait_send()

    barrier = pltpu.get_barrier_semaphore()
    for level in range(LEVELS):
        greet(across(level))
    pl.when(gives)(lambda: greet(relay_to))
    pl.when(takes)(lambda: greet(relay_from))

    loads = [
        pltpu.make_async_copy(src, dst, load_sem.at[i])
        for i, (src, dst) in enumerate(
            [
                (points_hbm, points),
                (leaf_index_hbm, leaf_index),
                (weights_hbm, weights),
                (node_index_hbm, node_index),
                (mask_hbm, mask),
            ]
        )
    ]
    start(loads)
    pl.semaphore_wait(barrier, LEVELS + gives.astype(jnp.int32) + takes.astype(jnp.int32))

    def remote(src, dst, send, recv, device):
        return pltpu.make_async_remote_copy(
            src_ref=src, dst_ref=dst, send_sem=send, recv_sem=recv,
            device_id=(device,), device_id_type=pl.DeviceIdType.MESH,
        )

    def x_copies(k):
        part = pl.ds(k * chunk, chunk)
        return [
            remote(points_hbm.at[part], near_x.at[0, part], x_send.at[k, 0], x_recv.at[k, 0], across(1)),
            remote(weights_hbm.at[part], near_w.at[0, part], x_send.at[k, 1], x_recv.at[k, 1], across(1)),
        ]

    def r_copies(k):
        part = pl.ds(k * chunk, chunk)
        return [
            remote(near_x.at[0, part], near_x.at[1, part], r_send.at[k, 0], r_recv.at[k, 0], relay_to),
            remote(near_w.at[0, part], near_w.at[1, part], r_send.at[k, 1], r_recv.at[k, 1], relay_to),
        ]

    def q_copies(k, slot):
        part = pl.ds(k * chunk, chunk)
        return [
            remote(near_x.at[slot, part], q_x.at[part], q_send.at[k, 0], q_recv.at[k, 0], across(0)),
            remote(near_w.at[slot, part], q_w.at[part], q_send.at[k, 1], q_recv.at[k, 1], across(0)),
        ]

    def s_copies():
        return [
            remote(points_hbm, sib_x, s_send.at[0], s_recv.at[0], across(0)),
            remote(weights_hbm, sib_w, s_send.at[1], s_recv.at[1], across(0)),
        ]

    def l_copy(level, kind):
        mine = (union_x, union_q)[kind].at[level, bit(level)]
        return remote(mine, mine, l_send.at[level, kind], l_recv.at[level, kind], across(level))

    def f_copy(level, kind):
        other = (union_x, union_q)[kind].at[level, 1 - bit(level)]
        return remote(other, other, f_send.at[level, kind], f_recv.at[level, kind], across(0))

    def tick(k):
        landed(x_copies(k))
        pl.when(gives)(lambda: start(r_copies(k)))
        pl.when(flip == 0)(lambda: start(q_copies(k, 0)))
        if k >= 2 and k + AHEAD < CHUNKS:
            start(x_copies(k + AHEAD))

    def relayed(k):
        @pl.when(takes)
        def _():
            landed(r_copies(k))
            pl.when(flip == 1)(lambda: start(q_copies(k, 1)))

    def crossed(k):
        pl.when(takes_q)(lambda: landed(q_copies(k, 0)))

    def reached(level, kind):
        if level == 0:
            landed([l_copy(level, kind)])
            return

        @pl.when(core == 1)
        def _():
            landed([l_copy(level, kind)])
            f_copy(level, kind).start()

    def whole(level):
        pl.when(core == 0)(lambda: landed([f_copy(level, kind) for kind in range(2)]))

    pending = []

    def flush():
        while pending:
            tile, w, at, column, first = pending.pop()
            value = dot(tile, w())
            if column is not None:
                value = jnp.where(mask[0, column] > 0, value, 0.0)
            if first:
                total[at, :] = value
            else:
                total[at, :] += value

    def product(right, w, column, first=False, blocks=range(BLOCKS)):
        for i in blocks:
            at = slice(i * block, (i + 1) * block)
            tile = affinity(own_left[at, :], right(), features).astype(jnp.bfloat16)
            flush()
            pending.append((tile, w, at, column, first))

    def near(x_ref, w_ref, a, b, column):
        part = slice(a * chunk, b * chunk)
        x = x_ref[part, :]
        other_right[part, :] = right_form(x, pieces(x))
        product(lambda: other_right[part, :], lambda: w_ref[part, :], column)

    def own(blocks):
        product(lambda: own_right[...], lambda: weights[...], None, True, blocks)

    sib_column = 2 * core

    def sib(blocks):
        if blocks[0] == 0:
            landed(s_copies())
            x = sib_x[...]
            other_right[...] = right_form(x, pieces(x))
        product(lambda: other_right[...], lambda: sib_w[...], sib_column, False, blocks)

    def beside(a, b):
        near(near_x.at[0], near_w.at[0], a, b, 1 + 2 * side)

    def beyond(a, b):
        near(near_x.at[1], near_w.at[1], a, b, 3 - 2 * side)

    def third(a, b):
        for k in range(a, b):
            crossed(k)
        near(q_x, q_w, a, b, 2 - 2 * core)

    def far(low, high):
        part = slice(low * skel, high * skel)
        for level in range(max(low, 1), high):
            whole(level)
        for level in range(low, high):
            at = slice(level * skel, (level + 1) * skel)
            p = union_x[level, 1 - bit(level)]
            far_right[at, :] = right_form(p, pieces(p))
            far_w[at, :] = union_q[level, 1 - bit(level)]
        product(lambda: far_right[part, :], lambda: far_w[part, :], None)

    def chosen(level, count):
        col = lax.broadcasted_iota(jnp.int32, (skel, count), 1).astype(jnp.float32)
        return jnp.where(col == indices[:, level : level + 1], 1.0, 0.0).astype(jnp.bfloat16)

    def climb_points(level):
        reached(level, 0)

        @pl.when(core == 1)
        def _():
            p = union_x[level].reshape(2 * skel, features)
            sk = dot(chosen(level + 1, 2 * skel), p).astype(jnp.bfloat16)
            union_x[level + 1, bit(level + 1)] = sk
            l_copy(level + 1, 0).start()
            aff = affinity(left_form(sk, pieces(sk)), right_form(p, pieces(p)), features)
            share[level] = (aff / jnp.sum(aff, axis=0, keepdims=True)).astype(jnp.bfloat16)

    def climb_charges(level):
        reached(level, 1)

        @pl.when(core == 1)
        def _():
            q = union_q[level].reshape(2 * skel, -1)
            union_q[level + 1, bit(level + 1)] = dot(share[level], q).astype(jnp.bfloat16)
            l_copy(level + 1, 1).start()

    start(x_copies(0))

    for load in (loads[0], loads[1], loads[3], loads[4]):
        load.wait()
    table = [leaf_index[...]] + [node_index[level] for level in range(LEVELS - 1)]
    table = jnp.concatenate(table + [table[0]] * (8 - LEVELS), axis=0)
    indices[...] = table.astype(jnp.float32).T

    x = points[...]
    sk = dot(chosen(0, rows), x).astype(jnp.bfloat16)
    union_x[0, core] = sk
    l_copy(0, 0).start()
    start(x_copies(1) + s_copies())
    norms = pieces(x)
    own_right[...] = right_form(x, norms)
    tile = affinity(left_form(sk, pieces(sk)), own_right[...], features).astype(jnp.bfloat16)
    loads[2].wait()
    union_q[0, core] = dot(tile, weights[...]).astype(jnp.bfloat16)
    l_copy(0, 1).start()

    climb_points(0)
    tick(0)
    own_left[...] = left_form(x, norms)
    climb_charges(0)
    for k in range(2, 2 + AHEAD):
        start(x_copies(k))
    own([0, 1])
    tick(1)
    own([2, 3])
    relayed(0)
    own([4, 5])
    climb_points(1)
    sib([0, 1])
    tick(2)
    relayed(1)
    climb_charges(1)
    sib([2, 3])
    tick(3)
    climb_points(2)
    relayed(2)
    sib([4, 5])
    tick(4)
    beside(0, 4)
    climb_charges(2)
    relayed(3)
    far(0, 1)
    tick(5)
    climb_points(3)
    beyond(0, 4)
    relayed(4)
    tick(6)
    third(0, 4)
    relayed(5)
    tick(7)
    climb_charges(3)
    far(1, 3)
    relayed(6)
    tick(8)
    beside(4, 8)
    reached(4, 0)
    relayed(7)
    tick(9)
    beyond(4, 8)
    relayed(8)
    tick(10)
    reached(4, 1)
    third(4, 8)
    relayed(9)
    tick(11)
    beside(8, 12)
    relayed(10)
    far(3, 5)
    relayed(11)
    beyond(8, 12)
    third(8, 12)
    flush()

    left_behind(s_copies())
    for k in range(CHUNKS):
        left_behind(x_copies(k))
    left_behind([l_copy(0, kind) for kind in range(2)])

    @pl.when(core == 1)
    def _():
        for level in range(1, LEVELS):
            left_behind([copy(level, kind) for copy in (l_copy, f_copy) for kind in range(2)])


    @pl.when(gives)
    def _():
        for k in range(CHUNKS):
            left_behind(r_copies(k))

    @pl.when((flip == 0) | takes)
    def _():
        for k in range(CHUNKS):
            left_behind(q_copies(k, 0))


def local(n, points, weights, targets, near_mask, leaf_skeleton, node_skeleton):
    rows, features = points.shape
    rhs = weights.shape[1]
    skel = leaf_skeleton.shape[1]
    vmem = pltpu.VMEM
    dma = pltpu.SemaphoreType.DMA
    bf16 = jnp.bfloat16
    hbm = pl.BlockSpec(memory_space=pltpu.HBM)
    total = pl.pallas_call(
        functools.partial(step, n),
        out_shape=jax.ShapeDtypeStruct((rows, rhs), jnp.float32),
        in_specs=[hbm] * 5,
        out_specs=pl.BlockSpec(memory_space=vmem),
        scratch_shapes=[
            pltpu.SMEM(near_mask.shape, jnp.int32),
            vmem(points.shape, bf16),
            vmem(weights.shape, bf16),
            vmem(leaf_skeleton.shape, jnp.int32),
            vmem(node_skeleton.shape, jnp.int32),
            vmem((2, rows, features), bf16),
            vmem((2, rows, rhs), bf16),
            vmem((rows, features), bf16),
            vmem((rows, rhs), bf16),
            vmem((rows, features), bf16),
            vmem((rows, rhs), bf16),
            vmem((LEVELS, 2, skel, features), bf16),
            vmem((LEVELS, 2, skel, rhs), bf16),
            vmem((LEVELS - 1, skel, 2 * skel), bf16),
            vmem((rows, 2 * features), bf16),
            vmem((rows, 2 * features), bf16),
            vmem((rows, 2 * features), bf16),
            vmem((LEVELS * skel, 2 * features), bf16),
            vmem((LEVELS * skel, rhs), bf16),
            vmem((skel, 8), jnp.float32),
            dma((5,)),
            dma((CHUNKS, 2)),
            dma((CHUNKS, 2)),
            dma((CHUNKS, 2)),
            dma((CHUNKS, 2)),
            dma((CHUNKS, 2)),
            dma((CHUNKS, 2)),
            dma((2,)),
            dma((2,)),
            dma((LEVELS, 2)),
            dma((LEVELS, 2)),
            dma((LEVELS, 2)),
            dma((LEVELS, 2)),
        ],
        compiler_params=pltpu.CompilerParams(
            collective_id=0, has_side_effects=True, vmem_limit_bytes=60 * 1024 * 1024
        ),
    )(near_mask, points, weights, leaf_skeleton, node_skeleton)
    wide = weights.astype(jnp.float32)
    residual = targets.astype(jnp.float32) - ridge_weight * wide - total
    updated = (wide + damping * residual / (1.0 + ridge_weight)).astype(jnp.bfloat16)
    return updated, residual


def solution(mesh):
    placed = (
        P("leaf", None),
        P("leaf", None),
        P("leaf", None),
        P("leaf", None),
        P("leaf", None),
        P(None, "leaf", None),
    )
    return jax.shard_map(
        functools.partial(local, mesh.shape["leaf"]),
        mesh=mesh,
        in_specs=placed,
        out_specs=(P("leaf", None), P("leaf", None)),
        check_vma=False,
    )
```

```python
import functools

import jax
import jax.numpy as jnp
from jax import lax
from jax.experimental import pallas as pl
from jax.experimental.pallas import tpu as pltpu
from jax.sharding import PartitionSpec as P

LEVELS = 5

ridge_weight = 1.0
damping = 0.25
LOG2E = 1.4426950408889634

GRAINS = 24
EDGES = (0, 1, 2, 4, 6, 8, 10, 12, 14, 16, 18, 20, 22, 23, 24)
CHUNKS = len(EDGES) - 1
BLOCKS = 6
AHEAD = 3

def pieces(rows):
    wide = rows.astype(jnp.float32)
    sq = jnp.sum(wide * wide, axis=1, keepdims=True)
    hi = sq.astype(jnp.bfloat16).astype(jnp.float32)
    rest = sq - hi
    mid = rest.astype(jnp.bfloat16).astype(jnp.float32)
    return hi, mid, rest - mid


def extra(rows, parts, first, second):
    hi, mid, low = parts
    lane = lax.broadcasted_iota(jnp.int32, rows.shape, 1)

    def picked(which, start):
        if which is None:
            return jnp.where((lane >= start) & (lane < start + 3), 1.0, 0.0)
        zero = jnp.zeros(rows.shape, jnp.float32)
        out = jnp.where(lane == start, hi, zero)
        out = jnp.where(lane == start + 1, mid, out)
        return jnp.where(lane == start + 2, low, out)

    return picked(first, 0) + picked(second, 3)


def left_form(rows, parts):
    tail = -extra(rows, parts, "norms", None)
    return jnp.concatenate(
        [(rows.astype(jnp.float32) * 2.0).astype(jnp.bfloat16), tail.astype(jnp.bfloat16)], axis=1
    )


def right_form(rows, parts):
    tail = extra(rows, parts, None, "norms")
    return jnp.concatenate([rows, tail.astype(jnp.bfloat16)], axis=1)


def affinity(left, right, features):
    s = lax.dot_general(left, right, (((1,), (1,)), ((), ())), preferred_element_type=jnp.float32)
    return jnp.exp2(s * (LOG2E / features))


def dot(a, b):
    return jnp.dot(a, b, preferred_element_type=jnp.float32)


def step(
    n,
    mask_hbm,
    points_hbm,
    weights_hbm,
    leaf_index_hbm,
    node_index_hbm,
    total,
    mask,
    points,
    weights,
    leaf_index,
    node_index,
    near_x,
    near_w,
    sib_x,
    sib_w,
    q_x,
    q_w,
    union_x,
    union_q,
    share,
    own_left,
    own_right,
    other_right,
    far_right,
    far_w,
    indices,
    load_sem,
    x_send,
    x_recv,
    r_send,
    r_recv,
    q_send,
    q_recv,
    s_send,
    s_recv,
    l_send,
    l_recv,
    f_send,
    f_recv,
    w_send,
    w_recv,
):
    me = lax.axis_index("leaf")
    rows, features = points.shape
    skel = leaf_index.shape[1]
    grain = rows // GRAINS
    block = rows // BLOCKS
    core = lax.rem(me, 2)
    side = lax.rem(me // 2, 2)
    flip = core + side - 2 * core * side
    relay_to = me + 4 - 8 * side
    relay_from = me - 4 + 8 * side
    gives = (relay_to >= 0) & (relay_to < n)
    takes = (relay_from >= 0) & (relay_from < n)
    takes_q = (flip == 1) | takes

    def bit(level):
        return lax.rem(me // (2**level), 2)

    def across(level):
        return me + (1 - 2 * bit(level)) * (2**level)

    top = LEVELS - 1
    inner = bit(top - 1) != bit(top)
    opposite = across(top) + across(top - 1) - me

    def greet(device):
        pl.semaphore_signal(barrier, inc=1, device_id=(device,), device_id_type=pl.DeviceIdType.MESH)

    def start(copies):
        for copy in copies:
            copy.start()

    def landed(copies):
        for copy in copies:
            copy.wait_recv()

    def left_behind(copies):
        for copy in copies:
            copy.wait_send()

    barrier = pltpu.get_barrier_semaphore()
    for level in range(LEVELS):
        greet(across(level))
    greet(opposite)
    pl.when(gives)(lambda: greet(relay_to))
    pl.when(takes)(lambda: greet(relay_from))

    loads = [
        pltpu.make_async_copy(src, dst, load_sem.at[i])
        for i, (src, dst) in enumerate(
            [
                (points_hbm, points),
                (leaf_index_hbm, leaf_index),
                (weights_hbm, weights),
                (node_index_hbm, node_index),
                (mask_hbm, mask),
            ]
        )
    ]
    start(loads)
    pl.semaphore_wait(barrier, LEVELS + 1 + gives.astype(jnp.int32) + takes.astype(jnp.int32))

    def remote(src, dst, send, recv, device):
        return pltpu.make_async_remote_copy(
            src_ref=src, dst_ref=dst, send_sem=send, recv_sem=recv,
            device_id=(device,), device_id_type=pl.DeviceIdType.MESH,
        )

    def x_copies(k):
        part = pl.ds(EDGES[k] * grain, (EDGES[k + 1] - EDGES[k]) * grain)
        return [
            remote(points_hbm.at[part], near_x.at[0, part], x_send.at[k, 0], x_recv.at[k, 0], across(1)),
            remote(weights_hbm.at[part], near_w.at[0, part], x_send.at[k, 1], x_recv.at[k, 1], across(1)),
        ]

    def r_copies(k):
        part = pl.ds(EDGES[k] * grain, (EDGES[k + 1] - EDGES[k]) * grain)
        return [
            remote(near_x.at[0, part], near_x.at[1, part], r_send.at[k, 0], r_recv.at[k, 0], relay_to),
            remote(near_w.at[0, part], near_w.at[1, part], r_send.at[k, 1], r_recv.at[k, 1], relay_to),
        ]

    def q_copies(k, slot):
        part = pl.ds(EDGES[k] * grain, (EDGES[k + 1] - EDGES[k]) * grain)
        return [
            remote(near_x.at[slot, part], q_x.at[part], q_send.at[k, 0], q_recv.at[k, 0], across(0)),
            remote(near_w.at[slot, part], q_w.at[part], q_send.at[k, 1], q_recv.at[k, 1], across(0)),
        ]

    def s_copies():
        return [
            remote(points_hbm, sib_x, s_send.at[0], s_recv.at[0], across(0)),
            remote(weights_hbm, sib_w, s_send.at[1], s_recv.at[1], across(0)),
        ]

    def l_copy(level, kind):
        mine = (union_x, union_q)[kind].at[level, bit(level)]
        to = opposite if level == top else across(level)
        return remote(mine, mine, l_send.at[level, kind], l_recv.at[level, kind], to)

    def w_copy(kind):
        other = (union_x, union_q)[kind].at[top, 1 - bit(top)]
        return remote(other, other, w_send.at[kind], w_recv.at[kind], across(top - 1))

    def f_copy(level, kind):
        other = (union_x, union_q)[kind].at[level, 1 - bit(level)]
        return remote(other, other, f_send.at[level, kind], f_recv.at[level, kind], across(0))

    def tick(k):
        landed(x_copies(k))
        pl.when(gives)(lambda: start(r_copies(k)))
        pl.when(flip == 0)(lambda: start(q_copies(k, 0)))
        if k >= 3 and k + AHEAD < CHUNKS:
            start(x_copies(k + AHEAD))

    def relayed(k):
        @pl.when(takes)
        def _():
            landed(r_copies(k))
            pl.when(flip == 1)(lambda: start(q_copies(k, 1)))

    def crossed(k):
        pl.when(takes_q)(lambda: landed(q_copies(k, 0)))

    def reached(level, kind):
        if level == 0:
            landed([l_copy(level, kind)])
            return

        @pl.when(core == 1)
        def _():
            landed([l_copy(level, kind)])
            f_copy(level, kind).start()

    def passed(kind):
        @pl.when((core == 1) & inner)
        def _():
            landed([l_copy(top, kind)])
            w_copy(kind).start()
            f_copy(top, kind).start()

    def ended(kind):
        @pl.when((core == 1) & ~inner)
        def _():
            landed([w_copy(kind)])
            f_copy(top, kind).start()

    def whole(level):
        pl.when(core == 0)(lambda: landed([f_copy(level, kind) for kind in range(2)]))

    pending = []

    def flush():
        while pending:
            tile, w, at, column, first = pending.pop()
            value = dot(tile, w())
            if column is not None:
                value = jnp.where(mask[0, column] > 0, value, 0.0)
            if first:
                total[at, :] = value
            else:
                total[at, :] += value

    def product(right, w, column, first=False, blocks=range(BLOCKS)):
        for i in blocks:
            at = slice(i * block, (i + 1) * block)
            tile = affinity(own_left[at, :], right(), features).astype(jnp.bfloat16)
            flush()
            pending.append((tile, w, at, column, first))

    def near(x_ref, w_ref, a, b, column):
        part = slice(EDGES[a] * grain, EDGES[b] * grain)
        x = x_ref[part, :]
        other_right[part, :] = right_form(x, pieces(x))
        product(lambda: other_right[part, :], lambda: w_ref[part, :], column)

    def own(blocks):
        product(lambda: own_right[...], lambda: weights[...], None, True, blocks)

    sib_column = 2 * core

    def sib(blocks):
        if blocks[0] == 0:
            landed(s_copies())
            x = sib_x[...]
            other_right[...] = right_form(x, pieces(x))
        product(lambda: other_right[...], lambda: sib_w[...], sib_column, False, blocks)

    def beside(a, b):
        near(near_x.at[0], near_w.at[0], a, b, 1 + 2 * side)

    def beyond(a, b):
        near(near_x.at[1], near_w.at[1], a, b, 3 - 2 * side)

    def third(a, b):
        for k in range(a, b):
            crossed(k)
        near(q_x, q_w, a, b, 2 - 2 * core)

    def far(low, high):
        part = slice(low * skel, high * skel)
        for level in range(max(low, 1), high):
            whole(level)
        for level in range(low, high):
            at = slice(level * skel, (level + 1) * skel)
            p = union_x[level, 1 - bit(level)]
            far_right[at, :] = right_form(p, pieces(p))
            far_w[at, :] = union_q[level, 1 - bit(level)]
        product(lambda: far_right[part, :], lambda: far_w[part, :], None)

    def chosen(level, count):
        col = lax.broadcasted_iota(jnp.int32, (skel, count), 1).astype(jnp.float32)
        return jnp.where(col == indices[:, level : level + 1], 1.0, 0.0).astype(jnp.bfloat16)

    def onward(level, kind):
        if level == top:
            pl.when(inner)(lambda: l_copy(level, kind).start())
        else:
            l_copy(level, kind).start()

    def climb_points(level):
        reached(level, 0)

        @pl.when(core == 1)
        def _():
            p = union_x[level].reshape(2 * skel, features)
            sk = dot(chosen(level + 1, 2 * skel), p).astype(jnp.bfloat16)
            union_x[level + 1, bit(level + 1)] = sk
            onward(level + 1, 0)
            aff = affinity(left_form(sk, pieces(sk)), right_form(p, pieces(p)), features)
            share[level] = (aff / jnp.sum(aff, axis=0, keepdims=True)).astype(jnp.bfloat16)

    def climb_charges(level):
        reached(level, 1)

        @pl.when(core == 1)
        def _():
            q = union_q[level].reshape(2 * skel, -1)
            union_q[level + 1, bit(level + 1)] = dot(share[level], q).astype(jnp.bfloat16)
            onward(level + 1, 1)

    start(x_copies(0) + x_copies(1))

    for load in (loads[0], loads[1], loads[3], loads[4]):
        load.wait()
    table = [leaf_index[...]] + [node_index[level] for level in range(LEVELS - 1)]
    table = jnp.concatenate(table + [table[0]] * (8 - LEVELS), axis=0)
    indices[...] = table.astype(jnp.float32).T

    x = points[...]
    sk = dot(chosen(0, rows), x).astype(jnp.bfloat16)
    union_x[0, core] = sk
    l_copy(0, 0).start()
    start(x_copies(2) + s_copies())
    norms = pieces(x)
    own_right[...] = right_form(x, norms)
    tile = affinity(left_form(sk, pieces(sk)), own_right[...], features).astype(jnp.bfloat16)
    loads[2].wait()
    union_q[0, core] = dot(tile, weights[...]).astype(jnp.bfloat16)
    l_copy(0, 1).start()

    climb_points(0)
    tick(0)
    tick(1)
    own_left[...] = left_form(x, norms)
    climb_charges(0)
    for k in range(3, 3 + AHEAD):
        start(x_copies(k))
    own([0, 1])
    tick(2)
    own([2, 3])
    relayed(0)
    relayed(1)
    own([4, 5])
    climb_points(1)
    sib([0, 1])
    tick(3)
    relayed(2)
    climb_charges(1)
    sib([2, 3])
    tick(4)
    climb_points(2)
    relayed(3)
    sib([4, 5])
    tick(5)
    beside(0, 5)
    climb_charges(2)
    relayed(4)
    far(0, 1)
    tick(6)
    climb_points(3)
    beyond(0, 5)
    relayed(5)
    tick(7)
    third(0, 5)
    relayed(6)
    tick(8)
    climb_charges(3)
    far(1, 3)
    relayed(7)
    tick(9)
    beside(5, 9)
    passed(0)
    relayed(8)
    tick(10)
    beyond(5, 9)
    relayed(9)
    tick(11)
    passed(1)
    third(5, 9)
    relayed(10)
    tick(12)
    beside(9, 11)
    tick(13)
    far(3, 4)
    relayed(11)
    beside(11, 14)
    ended(0)
    ended(1)
    relayed(12)
    beyond(9, 11)
    third(9, 11)
    relayed(13)
    far(4, 5)
    beyond(11, 14)
    third(11, 14)
    flush()

    left_behind(s_copies())
    for k in range(CHUNKS):
        left_behind(x_copies(k))
    left_behind([l_copy(0, kind) for kind in range(2)])

    @pl.when(core == 1)
    def _():
        for kind in range(2):
            left_behind([l_copy(level, kind) for level in range(1, top)])
            left_behind([f_copy(level, kind) for level in range(1, LEVELS)])
            pl.when(inner)(lambda: left_behind([l_copy(top, kind), w_copy(kind)]))


    @pl.when(gives)
    def _():
        for k in range(CHUNKS):
            left_behind(r_copies(k))

    @pl.when((flip == 0) | takes)
    def _():
        for k in range(CHUNKS):
            left_behind(q_copies(k, 0))


def local(n, points, weights, targets, near_mask, leaf_skeleton, node_skeleton):
    rows, features = points.shape
    rhs = weights.shape[1]
    skel = leaf_skeleton.shape[1]
    vmem = pltpu.VMEM
    dma = pltpu.SemaphoreType.DMA
    bf16 = jnp.bfloat16
    hbm = pl.BlockSpec(memory_space=pltpu.HBM)
    total = pl.pallas_call(
        functools.partial(step, n),
        out_shape=pltpu.VMEM((rows, rhs), jnp.float32),
        in_specs=[hbm] * 5,
        out_specs=pl.BlockSpec(memory_space=vmem),
        scratch_shapes=[
            pltpu.SMEM(near_mask.shape, jnp.int32),
            vmem(points.shape, bf16),
            vmem(weights.shape, bf16),
            vmem(leaf_skeleton.shape, jnp.int32),
            vmem(node_skeleton.shape, jnp.int32),
            vmem((2, rows, features), bf16),
            vmem((2, rows, rhs), bf16),
            vmem((rows, features), bf16),
            vmem((rows, rhs), bf16),
            vmem((rows, features), bf16),
            vmem((rows, rhs), bf16),
            vmem((LEVELS, 2, skel, features), bf16),
            vmem((LEVELS, 2, skel, rhs), bf16),
            vmem((LEVELS - 1, skel, 2 * skel), bf16),
            vmem((rows, 2 * features), bf16),
            vmem((rows, 2 * features), bf16),
            vmem((rows, 2 * features), bf16),
            vmem((LEVELS * skel, 2 * features), bf16),
            vmem((LEVELS * skel, rhs), bf16),
            vmem((skel, 8), jnp.float32),
            dma((5,)),
            dma((CHUNKS, 2)),
            dma((CHUNKS, 2)),
            dma((CHUNKS, 2)),
            dma((CHUNKS, 2)),
            dma((CHUNKS, 2)),
            dma((CHUNKS, 2)),
            dma((2,)),
            dma((2,)),
            dma((LEVELS, 2)),
            dma((LEVELS, 2)),
            dma((LEVELS, 2)),
            dma((LEVELS, 2)),
            dma((2,)),
            dma((2,)),
        ],
        compiler_params=pltpu.CompilerParams(
            collective_id=0, has_side_effects=True, vmem_limit_bytes=60 * 1024 * 1024
        ),
    )(near_mask, points, weights, leaf_skeleton, node_skeleton)
    wide = weights.astype(jnp.float32)
    residual = targets.astype(jnp.float32) - ridge_weight * wide - total
    updated = (wide + damping * residual / (1.0 + ridge_weight)).astype(jnp.bfloat16)
    return updated, residual


def solution(mesh):
    placed = (
        P("leaf", None),
        P("leaf", None),
        P("leaf", None),
        P("leaf", None),
        P("leaf", None),
        P(None, "leaf", None),
    )
    return jax.shard_map(
        functools.partial(local, mesh.shape["leaf"]),
        mesh=mesh,
        in_specs=placed,
        out_specs=(P("leaf", None), P("leaf", None)),
        check_vma=False,
    )
```

```python
import functools

import jax
import jax.numpy as jnp
from jax import lax
from jax.experimental import pallas as pl
from jax.experimental.pallas import tpu as pltpu
from jax.sharding import PartitionSpec as P

LEVELS = 5

ridge_weight = 1.0
damping = 0.25
LOG2E = 1.4426950408889634

GRAINS = 24
EDGES = (0, 1, 2, 4, 6, 8, 10, 12, 14, 16, 18, 20, 22, 23, 24)
CHUNKS = len(EDGES) - 1
BLOCKS = 6
HELD = 3

def pieces(rows):
    wide = rows.astype(jnp.float32)
    sq = jnp.sum(wide * wide, axis=1, keepdims=True)
    hi = sq.astype(jnp.bfloat16).astype(jnp.float32)
    rest = sq - hi
    mid = rest.astype(jnp.bfloat16).astype(jnp.float32)
    return hi, mid, rest - mid


def extra(rows, parts, first, second):
    hi, mid, low = parts
    lane = lax.broadcasted_iota(jnp.int32, rows.shape, 1)

    def picked(which, start):
        if which is None:
            return jnp.where((lane >= start) & (lane < start + 3), 1.0, 0.0)
        zero = jnp.zeros(rows.shape, jnp.float32)
        out = jnp.where(lane == start, hi, zero)
        out = jnp.where(lane == start + 1, mid, out)
        return jnp.where(lane == start + 2, low, out)

    return picked(first, 0) + picked(second, 3)


def left_form(rows, parts):
    tail = -extra(rows, parts, "norms", None)
    return jnp.concatenate(
        [(rows.astype(jnp.float32) * 2.0).astype(jnp.bfloat16), tail.astype(jnp.bfloat16)], axis=1
    )


def right_form(rows, parts):
    tail = extra(rows, parts, None, "norms")
    return jnp.concatenate([rows, tail.astype(jnp.bfloat16)], axis=1)


def affinity(left, right, features):
    s = lax.dot_general(left, right, (((1,), (1,)), ((), ())), preferred_element_type=jnp.float32)
    return jnp.exp2(s * (LOG2E / features))


def dot(a, b):
    return jnp.dot(a, b, preferred_element_type=jnp.float32)


def step(
    n,
    mask_hbm,
    points_hbm,
    weights_hbm,
    leaf_index_hbm,
    node_index_hbm,
    total,
    mask,
    points,
    weights,
    leaf_index,
    node_index,
    near_x,
    near_w,
    sib_x,
    sib_w,
    q_x,
    q_w,
    union_x,
    union_q,
    share,
    own_left,
    own_right,
    other_right,
    far_right,
    far_w,
    indices,
    load_sem,
    x_send,
    x_recv,
    r_send,
    r_recv,
    q_send,
    q_recv,
    s_send,
    s_recv,
    l_send,
    l_recv,
    f_send,
    f_recv,
    w_send,
    w_recv,
):
    me = lax.axis_index("leaf")
    rows, features = points.shape
    skel = leaf_index.shape[1]
    grain = rows // GRAINS
    block = rows // BLOCKS
    core = lax.rem(me, 2)
    side = lax.rem(me // 2, 2)
    flip = core + side - 2 * core * side
    relay_to = me + 4 - 8 * side
    relay_from = me - 4 + 8 * side
    gives = (relay_to >= 0) & (relay_to < n)
    takes = (relay_from >= 0) & (relay_from < n)
    takes_q = (flip == 1) | takes

    def bit(level):
        return lax.rem(me // (2**level), 2)

    def across(level):
        return me + (1 - 2 * bit(level)) * (2**level)

    top = LEVELS - 1
    inner = bit(top - 1) != bit(top)
    opposite = across(top) + across(top - 1) - me

    def greet(device):
        pl.semaphore_signal(barrier, inc=1, device_id=(device,), device_id_type=pl.DeviceIdType.MESH)

    def start(copies):
        for copy in copies:
            copy.start()

    def landed(copies):
        for copy in copies:
            copy.wait_recv()

    def left_behind(copies):
        for copy in copies:
            copy.wait_send()

    barrier = pltpu.get_barrier_semaphore()
    for level in range(LEVELS):
        greet(across(level))
    greet(opposite)
    pl.when(gives)(lambda: greet(relay_to))
    pl.when(takes)(lambda: greet(relay_from))

    loads = [
        pltpu.make_async_copy(src, dst, load_sem.at[i])
        for i, (src, dst) in enumerate(
            [
                (points_hbm, points),
                (leaf_index_hbm, leaf_index),
                (weights_hbm, weights),
                (node_index_hbm, node_index),
                (mask_hbm, mask),
            ]
        )
    ]
    start(loads)
    pl.semaphore_wait(barrier, LEVELS + 1 + gives.astype(jnp.int32) + takes.astype(jnp.int32))

    def remote(src, dst, send, recv, device):
        return pltpu.make_async_remote_copy(
            src_ref=src, dst_ref=dst, send_sem=send, recv_sem=recv,
            device_id=(device,), device_id_type=pl.DeviceIdType.MESH,
        )

    def x_copies(k):
        part = pl.ds(EDGES[k] * grain, (EDGES[k + 1] - EDGES[k]) * grain)
        return [
            remote(points_hbm.at[part], near_x.at[0, part], x_send.at[k, 0], x_recv.at[k, 0], across(1)),
            remote(weights_hbm.at[part], near_w.at[0, part], x_send.at[k, 1], x_recv.at[k, 1], across(1)),
        ]

    def r_copies(k):
        part = pl.ds(EDGES[k] * grain, (EDGES[k + 1] - EDGES[k]) * grain)
        return [
            remote(near_x.at[0, part], near_x.at[1, part], r_send.at[k, 0], r_recv.at[k, 0], relay_to),
            remote(near_w.at[0, part], near_w.at[1, part], r_send.at[k, 1], r_recv.at[k, 1], relay_to),
        ]

    def q_copies(k, slot):
        part = pl.ds(EDGES[k] * grain, (EDGES[k + 1] - EDGES[k]) * grain)
        return [
            remote(near_x.at[slot, part], q_x.at[part], q_send.at[k, 0], q_recv.at[k, 0], across(0)),
            remote(near_w.at[slot, part], q_w.at[part], q_send.at[k, 1], q_recv.at[k, 1], across(0)),
        ]

    def s_copies():
        return [
            remote(points_hbm, sib_x, s_send.at[0], s_recv.at[0], across(0)),
            remote(weights_hbm, sib_w, s_send.at[1], s_recv.at[1], across(0)),
        ]

    def l_copy(level, kind):
        mine = (union_x, union_q)[kind].at[level, bit(level)]
        to = opposite if level == top else across(level)
        return remote(mine, mine, l_send.at[level, kind], l_recv.at[level, kind], to)

    def w_copy(kind):
        other = (union_x, union_q)[kind].at[top, 1 - bit(top)]
        return remote(other, other, w_send.at[kind], w_recv.at[kind], across(top - 1))

    def f_copy(level, kind):
        other = (union_x, union_q)[kind].at[level, 1 - bit(level)]
        return remote(other, other, f_send.at[level, kind], f_recv.at[level, kind], across(0))

    def tick(k):
        landed(x_copies(k))
        pl.when(gives)(lambda: start(r_copies(k)))
        pl.when(flip == 0)(lambda: start(q_copies(k, 0)))

    def relayed(k):
        @pl.when(takes)
        def _():
            landed(r_copies(k))
            pl.when(flip == 1)(lambda: start(q_copies(k, 1)))

    def crossed(k):
        pl.when(takes_q)(lambda: landed(q_copies(k, 0)))

    def reached(level, kind):
        if level == 0:
            landed([l_copy(level, kind)])
            return

        @pl.when(core == 1)
        def _():
            landed([l_copy(level, kind)])
            f_copy(level, kind).start()

    def passed(kind):
        @pl.when((core == 1) & inner)
        def _():
            landed([l_copy(top, kind)])
            w_copy(kind).start()
            f_copy(top, kind).start()

    def ended(kind):
        @pl.when((core == 1) & ~inner)
        def _():
            landed([w_copy(kind)])
            f_copy(top, kind).start()

    def whole(level):
        pl.when(core == 0)(lambda: landed([f_copy(level, kind) for kind in range(2)]))

    pending = []

    def flush():
        while pending:
            tile, w, at, column, first = pending.pop()
            value = dot(tile, w())
            if column is not None:
                value = jnp.where(mask[0, column] > 0, value, 0.0)
            if first:
                total[at, :] = value
            else:
                total[at, :] += value

    def product(right, w, column, first=False, blocks=range(BLOCKS)):
        for i in blocks:
            at = slice(i * block, (i + 1) * block)
            tile = affinity(own_left[at, :], right(), features).astype(jnp.bfloat16)
            flush()
            pending.append((tile, w, at, column, first))

    def near(x_ref, w_ref, a, b, column):
        part = slice(EDGES[a] * grain, EDGES[b] * grain)
        x = x_ref[part, :]
        other_right[part, :] = right_form(x, pieces(x))
        product(lambda: other_right[part, :], lambda: w_ref[part, :], column)

    def own(blocks):
        product(lambda: own_right[...], lambda: weights[...], None, True, blocks)

    sib_column = 2 * core

    def sib(blocks):
        if blocks[0] == 0:
            landed(s_copies())
            x = sib_x[...]
            other_right[...] = right_form(x, pieces(x))
        product(lambda: other_right[...], lambda: sib_w[...], sib_column, False, blocks)

    def beside(a, b):
        near(near_x.at[0], near_w.at[0], a, b, 1 + 2 * side)

    def beyond(a, b):
        near(near_x.at[1], near_w.at[1], a, b, 3 - 2 * side)

    def third(a, b):
        for k in range(a, b):
            crossed(k)
        near(q_x, q_w, a, b, 2 - 2 * core)

    def far(low, high):
        part = slice(low * skel, high * skel)
        for level in range(max(low, 1), high):
            whole(level)
        for level in range(low, high):
            at = slice(level * skel, (level + 1) * skel)
            p = union_x[level, 1 - bit(level)]
            far_right[at, :] = right_form(p, pieces(p))
            far_w[at, :] = union_q[level, 1 - bit(level)]
        product(lambda: far_right[part, :], lambda: far_w[part, :], None)

    def chosen(level, count):
        col = lax.broadcasted_iota(jnp.int32, (skel, count), 1).astype(jnp.float32)
        return jnp.where(col == indices[:, level : level + 1], 1.0, 0.0).astype(jnp.bfloat16)

    def onward(level, kind):
        if level == top:
            pl.when(inner)(lambda: l_copy(level, kind).start())
        else:
            l_copy(level, kind).start()

    def climb_points(level):
        reached(level, 0)

        @pl.when(core == 1)
        def _():
            p = union_x[level].reshape(2 * skel, features)
            sk = dot(chosen(level + 1, 2 * skel), p).astype(jnp.bfloat16)
            union_x[level + 1, bit(level + 1)] = sk
            onward(level + 1, 0)
            aff = affinity(left_form(sk, pieces(sk)), right_form(p, pieces(p)), features)
            share[level] = (aff / jnp.sum(aff, axis=0, keepdims=True)).astype(jnp.bfloat16)

    def climb_charges(level):
        reached(level, 1)

        @pl.when(core == 1)
        def _():
            q = union_q[level].reshape(2 * skel, -1)
            union_q[level + 1, bit(level + 1)] = dot(share[level], q).astype(jnp.bfloat16)
            onward(level + 1, 1)

    start(x_copies(0) + x_copies(1))

    for load in (loads[0], loads[1], loads[3], loads[4]):
        load.wait()
    table = [leaf_index[...]] + [node_index[level] for level in range(LEVELS - 1)]
    table = jnp.concatenate(table + [table[0]] * (8 - LEVELS), axis=0)
    indices[...] = table.astype(jnp.float32).T

    x = points[...]
    sk = dot(chosen(0, rows), x).astype(jnp.bfloat16)
    union_x[0, core] = sk
    l_copy(0, 0).start()
    for k in range(2, HELD):
        start(x_copies(k))
    start(s_copies())
    norms = pieces(x)
    own_right[...] = right_form(x, norms)
    tile = affinity(left_form(sk, pieces(sk)), own_right[...], features).astype(jnp.bfloat16)
    loads[2].wait()
    union_q[0, core] = dot(tile, weights[...]).astype(jnp.bfloat16)
    l_copy(0, 1).start()

    climb_points(0)
    tick(0)
    tick(1)
    own_left[...] = left_form(x, norms)
    climb_charges(0)
    for k in range(HELD, CHUNKS):
        start(x_copies(k))
    own([0, 1])
    tick(2)
    own([2, 3])
    relayed(0)
    relayed(1)
    own([4, 5])
    climb_points(1)
    sib([0, 1])
    tick(3)
    relayed(2)
    climb_charges(1)
    sib([2, 3])
    tick(4)
    climb_points(2)
    relayed(3)
    sib([4, 5])
    tick(5)
    beside(0, 5)
    climb_charges(2)
    relayed(4)
    far(0, 1)
    tick(6)
    climb_points(3)
    beyond(0, 5)
    relayed(5)
    tick(7)
    third(0, 5)
    relayed(6)
    tick(8)
    climb_charges(3)
    beside(5, 9)
    relayed(7)
    tick(9)
    far(1, 3)
    passed(0)
    relayed(8)
    tick(10)
    beyond(5, 9)
    relayed(9)
    tick(11)
    passed(1)
    third(5, 9)
    relayed(10)
    tick(12)
    beside(9, 11)
    beyond(9, 11)
    tick(13)
    far(3, 4)
    relayed(11)
    third(9, 11)
    beside(11, 14)
    ended(0)
    ended(1)
    relayed(12)
    relayed(13)
    far(4, 5)
    beyond(11, 14)
    third(11, 14)
    flush()

    left_behind(s_copies())
    for k in range(CHUNKS):
        left_behind(x_copies(k))
    left_behind([l_copy(0, kind) for kind in range(2)])

    @pl.when(core == 1)
    def _():
        for kind in range(2):
            left_behind([l_copy(level, kind) for level in range(1, top)])
            left_behind([f_copy(level, kind) for level in range(1, LEVELS)])
            pl.when(inner)(lambda: left_behind([l_copy(top, kind), w_copy(kind)]))


    @pl.when(gives)
    def _():
        for k in range(CHUNKS):
            left_behind(r_copies(k))

    @pl.when((flip == 0) | takes)
    def _():
        for k in range(CHUNKS):
            left_behind(q_copies(k, 0))


def finish(total, weights, targets, updated_hbm, residual_hbm, updated, residual, sem):
    block = total.shape[0] // BLOCKS
    copies = []
    for i in range(BLOCKS):
        at = pl.ds(i * block, block)
        wide = weights[at, :].astype(jnp.float32)
        rest = targets[at, :].astype(jnp.float32) - ridge_weight * wide - total[at, :]
        residual[at, :] = rest
        updated[at, :] = (wide + damping * rest / (1.0 + ridge_weight)).astype(jnp.bfloat16)
        copies.append(pltpu.make_async_copy(residual.at[at], residual_hbm.at[at], sem.at[0, i]))
        copies.append(pltpu.make_async_copy(updated.at[at], updated_hbm.at[at], sem.at[1, i]))
        copies[-2].start()
        copies[-1].start()
    for copy in copies:
        copy.wait()


def local(n, points, weights, targets, near_mask, leaf_skeleton, node_skeleton):
    rows, features = points.shape
    rhs = weights.shape[1]
    skel = leaf_skeleton.shape[1]
    vmem = pltpu.VMEM
    dma = pltpu.SemaphoreType.DMA
    bf16 = jnp.bfloat16
    hbm = pl.BlockSpec(memory_space=pltpu.HBM)
    total = pl.pallas_call(
        functools.partial(step, n),
        out_shape=pltpu.VMEM((rows, rhs), jnp.float32),
        in_specs=[hbm] * 5,
        out_specs=pl.BlockSpec(memory_space=vmem),
        scratch_shapes=[
            pltpu.SMEM(near_mask.shape, jnp.int32),
            vmem(points.shape, bf16),
            vmem(weights.shape, bf16),
            vmem(leaf_skeleton.shape, jnp.int32),
            vmem(node_skeleton.shape, jnp.int32),
            vmem((2, rows, features), bf16),
            vmem((2, rows, rhs), bf16),
            vmem((rows, features), bf16),
            vmem((rows, rhs), bf16),
            vmem((rows, features), bf16),
            vmem((rows, rhs), bf16),
            vmem((LEVELS, 2, skel, features), bf16),
            vmem((LEVELS, 2, skel, rhs), bf16),
            vmem((LEVELS - 1, skel, 2 * skel), bf16),
            vmem((rows, 2 * features), bf16),
            vmem((rows, 2 * features), bf16),
            vmem((rows, 2 * features), bf16),
            vmem((LEVELS * skel, 2 * features), bf16),
            vmem((LEVELS * skel, rhs), bf16),
            vmem((skel, 8), jnp.float32),
            dma((5,)),
            dma((CHUNKS, 2)),
            dma((CHUNKS, 2)),
            dma((CHUNKS, 2)),
            dma((CHUNKS, 2)),
            dma((CHUNKS, 2)),
            dma((CHUNKS, 2)),
            dma((2,)),
            dma((2,)),
            dma((LEVELS, 2)),
            dma((LEVELS, 2)),
            dma((LEVELS, 2)),
            dma((LEVELS, 2)),
            dma((2,)),
            dma((2,)),
        ],
        compiler_params=pltpu.CompilerParams(
            collective_id=0, has_side_effects=True, vmem_limit_bytes=60 * 1024 * 1024
        ),
    )(near_mask, points, weights, leaf_skeleton, node_skeleton)
    out = [jax.ShapeDtypeStruct((rows, rhs), bf16), jax.ShapeDtypeStruct((rows, rhs), jnp.float32)]
    every = pl.BlockSpec(memory_space=vmem)
    return pl.pallas_call(
        finish,
        out_shape=out,
        in_specs=[every] * 3,
        out_specs=[hbm] * 2,
        scratch_shapes=[
            vmem((rows, rhs), bf16),
            vmem((rows, rhs), jnp.float32),
            dma((2, BLOCKS)),
        ],
        compiler_params=pltpu.CompilerParams(vmem_limit_bytes=16 * 1024 * 1024),
    )(total, weights, targets)


def solution(mesh):
    placed = (
        P("leaf", None),
        P("leaf", None),
        P("leaf", None),
        P("leaf", None),
        P("leaf", None),
        P(None, "leaf", None),
    )
    return jax.shard_map(
        functools.partial(local, mesh.shape["leaf"]),
        mesh=mesh,
        in_specs=placed,
        out_specs=(P("leaf", None), P("leaf", None)),
        check_vma=False,
    )
```

```python
import functools

import jax
import jax.numpy as jnp
from jax import lax
from jax.experimental import pallas as pl
from jax.experimental.pallas import tpu as pltpu
from jax.sharding import PartitionSpec as P

LEVELS = 5

ridge_weight = 1.0
damping = 0.25
LOG2E = 1.4426950408889634

GRAINS = 24
EDGES = (0, 1, 2, 4, 6, 8, 10, 12, 14, 16, 18, 20, 22, 23, 24)
CHUNKS = len(EDGES) - 1
BLOCKS = 6
HELD = 3

def pieces(rows):
    wide = rows.astype(jnp.float32)
    sq = jnp.sum(wide * wide, axis=1, keepdims=True)
    hi = sq.astype(jnp.bfloat16).astype(jnp.float32)
    rest = sq - hi
    mid = rest.astype(jnp.bfloat16).astype(jnp.float32)
    return hi, mid, rest - mid


def extra(rows, parts, first, second):
    hi, mid, low = parts
    lane = lax.broadcasted_iota(jnp.int32, rows.shape, 1)

    def picked(which, start):
        if which is None:
            return jnp.where((lane >= start) & (lane < start + 3), 1.0, 0.0)
        zero = jnp.zeros(rows.shape, jnp.float32)
        out = jnp.where(lane == start, hi, zero)
        out = jnp.where(lane == start + 1, mid, out)
        return jnp.where(lane == start + 2, low, out)

    return picked(first, 0) + picked(second, 3)


def left_form(rows, parts):
    tail = -extra(rows, parts, "norms", None)
    return jnp.concatenate(
        [(rows.astype(jnp.float32) * 2.0).astype(jnp.bfloat16), tail.astype(jnp.bfloat16)], axis=1
    )


def right_form(rows, parts):
    tail = extra(rows, parts, None, "norms")
    return jnp.concatenate([rows, tail.astype(jnp.bfloat16)], axis=1)


def affinity(left, right, features):
    s = lax.dot_general(left, right, (((1,), (1,)), ((), ())), preferred_element_type=jnp.float32)
    return jnp.exp2(s * (LOG2E / features))


def dot(a, b):
    return jnp.dot(a, b, preferred_element_type=jnp.float32)


def step(
    n,
    mask_hbm,
    points_hbm,
    weights_hbm,
    leaf_index_hbm,
    node_index_hbm,
    total,
    mask,
    points,
    weights,
    leaf_index,
    node_index,
    near_x,
    near_w,
    sib_x,
    sib_w,
    q_x,
    q_w,
    union_x,
    union_q,
    share,
    own_left,
    own_right,
    other_right,
    far_right,
    far_w,
    indices,
    load_sem,
    x_send,
    x_recv,
    r_send,
    r_recv,
    q_send,
    q_recv,
    s_send,
    s_recv,
    l_send,
    l_recv,
    f_send,
    f_recv,
    w_send,
    w_recv,
):
    me = lax.axis_index("leaf")
    rows, features = points.shape
    skel = leaf_index.shape[1]
    grain = rows // GRAINS
    block = rows // BLOCKS
    core = lax.rem(me, 2)
    side = lax.rem(me // 2, 2)
    flip = core + side - 2 * core * side
    relay_to = me + 4 - 8 * side
    relay_from = me - 4 + 8 * side
    gives = (relay_to >= 0) & (relay_to < n)
    takes = (relay_from >= 0) & (relay_from < n)
    takes_q = (flip == 1) | takes

    def bit(level):
        return lax.rem(me // (2**level), 2)

    def across(level):
        return me + (1 - 2 * bit(level)) * (2**level)

    top = LEVELS - 1
    inner = bit(top - 1) != bit(top)
    opposite = across(top) + across(top - 1) - me

    def greet(device):
        pl.semaphore_signal(barrier, inc=1, device_id=(device,), device_id_type=pl.DeviceIdType.MESH)

    def start(copies):
        for copy in copies:
            copy.start()

    def landed(copies):
        for copy in copies:
            copy.wait_recv()

    def left_behind(copies):
        for copy in copies:
            copy.wait_send()

    barrier = pltpu.get_barrier_semaphore()
    for level in range(LEVELS):
        greet(across(level))
    greet(opposite)
    pl.when(gives)(lambda: greet(relay_to))
    pl.when(takes)(lambda: greet(relay_from))

    loads = [
        pltpu.make_async_copy(src, dst, load_sem.at[i])
        for i, (src, dst) in enumerate(
            [
                (points_hbm, points),
                (leaf_index_hbm, leaf_index),
                (weights_hbm, weights),
                (node_index_hbm, node_index),
                (mask_hbm, mask),
            ]
        )
    ]
    start(loads)
    pl.semaphore_wait(barrier, LEVELS + 1 + gives.astype(jnp.int32) + takes.astype(jnp.int32))

    def remote(src, dst, send, recv, device):
        return pltpu.make_async_remote_copy(
            src_ref=src, dst_ref=dst, send_sem=send, recv_sem=recv,
            device_id=(device,), device_id_type=pl.DeviceIdType.MESH,
        )

    def x_copies(k):
        part = pl.ds(EDGES[k] * grain, (EDGES[k + 1] - EDGES[k]) * grain)
        return [
            remote(points_hbm.at[part], near_x.at[0, part], x_send.at[k, 0], x_recv.at[k, 0], across(1)),
            remote(weights_hbm.at[part], near_w.at[0, part], x_send.at[k, 1], x_recv.at[k, 1], across(1)),
        ]

    def r_copies(k):
        part = pl.ds(EDGES[k] * grain, (EDGES[k + 1] - EDGES[k]) * grain)
        return [
            remote(near_x.at[0, part], near_x.at[1, part], r_send.at[k, 0], r_recv.at[k, 0], relay_to),
            remote(near_w.at[0, part], near_w.at[1, part], r_send.at[k, 1], r_recv.at[k, 1], relay_to),
        ]

    def q_copies(k, slot):
        part = pl.ds(EDGES[k] * grain, (EDGES[k + 1] - EDGES[k]) * grain)
        return [
            remote(near_x.at[slot, part], q_x.at[part], q_send.at[k, 0], q_recv.at[k, 0], across(0)),
            remote(near_w.at[slot, part], q_w.at[part], q_send.at[k, 1], q_recv.at[k, 1], across(0)),
        ]

    def s_copies():
        return [
            remote(points_hbm, sib_x, s_send.at[0], s_recv.at[0], across(0)),
            remote(weights_hbm, sib_w, s_send.at[1], s_recv.at[1], across(0)),
        ]

    def l_copy(level, kind):
        mine = (union_x, union_q)[kind].at[level, bit(level)]
        to = opposite if level == top else across(level)
        return remote(mine, mine, l_send.at[level, kind], l_recv.at[level, kind], to)

    def w_copy(kind):
        other = (union_x, union_q)[kind].at[top, 1 - bit(top)]
        return remote(other, other, w_send.at[kind], w_recv.at[kind], across(top - 1))

    def f_copy(level, kind):
        other = (union_x, union_q)[kind].at[level, 1 - bit(level)]
        return remote(other, other, f_send.at[level, kind], f_recv.at[level, kind], across(0))

    def tick(k):
        landed(x_copies(k))
        pl.when(gives)(lambda: start(r_copies(k)))
        pl.when(flip == 0)(lambda: start(q_copies(k, 0)))

    def relayed(k):
        @pl.when(takes)
        def _():
            landed(r_copies(k))
            pl.when(flip == 1)(lambda: start(q_copies(k, 1)))

    def crossed(k):
        pl.when(takes_q)(lambda: landed(q_copies(k, 0)))

    def reached(level, kind):
        if level == 0:
            landed([l_copy(level, kind)])
            return

        @pl.when(core == 1)
        def _():
            landed([l_copy(level, kind)])
            f_copy(level, kind).start()

    def passed(kind):
        @pl.when((core == 1) & inner)
        def _():
            landed([l_copy(top, kind)])
            w_copy(kind).start()
            f_copy(top, kind).start()

    def ended(kind):
        @pl.when((core == 1) & ~inner)
        def _():
            landed([w_copy(kind)])
            f_copy(top, kind).start()

    def whole(level):
        pl.when(core == 0)(lambda: landed([f_copy(level, kind) for kind in range(2)]))

    pending = []

    def flush():
        while pending:
            tile, w, at, column, first = pending.pop()
            value = dot(tile, w())
            if column is not None:
                value = jnp.where(mask[0, column] > 0, value, 0.0)
            if first:
                total[at, :] = value
            else:
                total[at, :] += value

    def product(right, w, column, first=False, blocks=range(BLOCKS)):
        for i in blocks:
            at = slice(i * block, (i + 1) * block)
            tile = affinity(own_left[at, :], right(), features).astype(jnp.bfloat16)
            flush()
            pending.append((tile, w, at, column, first))

    def near(x_ref, w_ref, a, b, column):
        part = slice(EDGES[a] * grain, EDGES[b] * grain)
        x = x_ref[part, :]
        other_right[part, :] = right_form(x, pieces(x))
        product(lambda: other_right[part, :], lambda: w_ref[part, :], column)

    def own(blocks):
        product(lambda: own_right[...], lambda: weights[...], None, True, blocks)

    sib_column = 2 * core

    def sib(blocks):
        if blocks[0] == 0:
            landed(s_copies())
            x = sib_x[...]
            other_right[...] = right_form(x, pieces(x))
        product(lambda: other_right[...], lambda: sib_w[...], sib_column, False, blocks)

    def beside(a, b):
        near(near_x.at[0], near_w.at[0], a, b, 1 + 2 * side)

    def beyond(a, b):
        near(near_x.at[1], near_w.at[1], a, b, 3 - 2 * side)

    def third(a, b):
        for k in range(a, b):
            crossed(k)
        near(q_x, q_w, a, b, 2 - 2 * core)

    def far(low, high):
        part = slice(low * skel, high * skel)
        for level in range(max(low, 1), high):
            whole(level)
        for level in range(low, high):
            at = slice(level * skel, (level + 1) * skel)
            p = union_x[level, 1 - bit(level)]
            far_right[at, :] = right_form(p, pieces(p))
            far_w[at, :] = union_q[level, 1 - bit(level)]
        product(lambda: far_right[part, :], lambda: far_w[part, :], None)

    def chosen(level, count):
        col = lax.broadcasted_iota(jnp.int32, (skel, count), 1).astype(jnp.float32)
        return jnp.where(col == indices[:, level : level + 1], 1.0, 0.0).astype(jnp.bfloat16)

    def onward(level, kind):
        if level == top:
            pl.when(inner)(lambda: l_copy(level, kind).start())
        else:
            l_copy(level, kind).start()

    def climb_points(level):
        reached(level, 0)

        @pl.when(core == 1)
        def _():
            p = union_x[level].reshape(2 * skel, features)
            sk = dot(chosen(level + 1, 2 * skel), p).astype(jnp.bfloat16)
            union_x[level + 1, bit(level + 1)] = sk
            onward(level + 1, 0)
            aff = affinity(left_form(sk, pieces(sk)), right_form(p, pieces(p)), features)
            share[level] = (aff / jnp.sum(aff, axis=0, keepdims=True)).astype(jnp.bfloat16)

    def climb_charges(level):
        reached(level, 1)

        @pl.when(core == 1)
        def _():
            q = union_q[level].reshape(2 * skel, -1)
            union_q[level + 1, bit(level + 1)] = dot(share[level], q).astype(jnp.bfloat16)
            onward(level + 1, 1)

    start(x_copies(0) + x_copies(1))

    for load in (loads[0], loads[1], loads[3], loads[4]):
        load.wait()
    table = [leaf_index[...]] + [node_index[level] for level in range(LEVELS - 1)]
    table = jnp.concatenate(table + [table[0]] * (8 - LEVELS), axis=0)
    indices[...] = table.astype(jnp.float32).T

    x = points[...]
    sk = dot(chosen(0, rows), x).astype(jnp.bfloat16)
    union_x[0, core] = sk
    l_copy(0, 0).start()
    for k in range(2, HELD):
        start(x_copies(k))
    start(s_copies())
    norms = pieces(x)
    own_right[...] = right_form(x, norms)
    tile = affinity(left_form(sk, pieces(sk)), own_right[...], features).astype(jnp.bfloat16)
    loads[2].wait()
    union_q[0, core] = dot(tile, weights[...]).astype(jnp.bfloat16)
    l_copy(0, 1).start()

    climb_points(0)
    tick(0)
    tick(1)
    own_left[...] = left_form(x, norms)
    climb_charges(0)
    for k in range(HELD, CHUNKS):
        start(x_copies(k))
    own([0, 1])
    tick(2)
    own([2, 3])
    relayed(0)
    relayed(1)
    own([4, 5])
    climb_points(1)
    sib([0, 1])
    tick(3)
    relayed(2)
    climb_charges(1)
    sib([2, 3])
    tick(4)
    climb_points(2)
    relayed(3)
    sib([4, 5])
    tick(5)
    beside(0, 5)
    climb_charges(2)
    relayed(4)
    far(0, 1)
    tick(6)
    climb_points(3)
    beyond(0, 5)
    relayed(5)
    tick(7)
    third(0, 5)
    relayed(6)
    tick(8)
    climb_charges(3)
    beside(5, 9)
    relayed(7)
    tick(9)
    far(1, 3)
    passed(0)
    relayed(8)
    tick(10)
    beyond(5, 9)
    relayed(9)
    tick(11)
    passed(1)
    third(5, 9)
    relayed(10)
    tick(12)
    beside(9, 11)
    beyond(9, 11)
    tick(13)
    far(3, 4)
    relayed(11)
    third(9, 11)
    beside(11, 14)
    relayed(12)
    ended(0)
    ended(1)
    relayed(13)
    far(4, 5)
    beyond(11, 14)
    third(11, 14)
    flush()

    left_behind(s_copies())
    for k in range(CHUNKS):
        left_behind(x_copies(k))
    left_behind([l_copy(0, kind) for kind in range(2)])

    @pl.when(core == 1)
    def _():
        for kind in range(2):
            left_behind([l_copy(level, kind) for level in range(1, top)])
            left_behind([f_copy(level, kind) for level in range(1, LEVELS)])
            pl.when(inner)(lambda: left_behind([l_copy(top, kind), w_copy(kind)]))


    @pl.when(gives)
    def _():
        for k in range(CHUNKS):
            left_behind(r_copies(k))

    @pl.when((flip == 0) | takes)
    def _():
        for k in range(CHUNKS):
            left_behind(q_copies(k, 0))


def finish(total, weights, targets, updated_hbm, residual_hbm, updated, residual, sem):
    block = total.shape[0] // BLOCKS
    copies = []
    for i in range(BLOCKS):
        at = pl.ds(i * block, block)
        wide = weights[at, :].astype(jnp.float32)
        rest = targets[at, :].astype(jnp.float32) - ridge_weight * wide - total[at, :]
        residual[at, :] = rest
        updated[at, :] = (wide + damping * rest / (1.0 + ridge_weight)).astype(jnp.bfloat16)
        copies.append(pltpu.make_async_copy(residual.at[at], residual_hbm.at[at], sem.at[0, i]))
        copies.append(pltpu.make_async_copy(updated.at[at], updated_hbm.at[at], sem.at[1, i]))
        copies[-2].start()
        copies[-1].start()
    for copy in copies:
        copy.wait()


def local(n, points, weights, targets, near_mask, leaf_skeleton, node_skeleton):
    rows, features = points.shape
    rhs = weights.shape[1]
    skel = leaf_skeleton.shape[1]
    vmem = pltpu.VMEM
    dma = pltpu.SemaphoreType.DMA
    bf16 = jnp.bfloat16
    hbm = pl.BlockSpec(memory_space=pltpu.HBM)
    total = pl.pallas_call(
        functools.partial(step, n),
        out_shape=pltpu.VMEM((rows, rhs), jnp.float32),
        in_specs=[hbm] * 5,
        out_specs=pl.BlockSpec(memory_space=vmem),
        scratch_shapes=[
            pltpu.SMEM(near_mask.shape, jnp.int32),
            vmem(points.shape, bf16),
            vmem(weights.shape, bf16),
            vmem(leaf_skeleton.shape, jnp.int32),
            vmem(node_skeleton.shape, jnp.int32),
            vmem((2, rows, features), bf16),
            vmem((2, rows, rhs), bf16),
            vmem((rows, features), bf16),
            vmem((rows, rhs), bf16),
            vmem((rows, features), bf16),
            vmem((rows, rhs), bf16),
            vmem((LEVELS, 2, skel, features), bf16),
            vmem((LEVELS, 2, skel, rhs), bf16),
            vmem((LEVELS - 1, skel, 2 * skel), bf16),
            vmem((rows, 2 * features), bf16),
            vmem((rows, 2 * features), bf16),
            vmem((rows, 2 * features), bf16),
            vmem((LEVELS * skel, 2 * features), bf16),
            vmem((LEVELS * skel, rhs), bf16),
            vmem((skel, 8), jnp.float32),
            dma((5,)),
            dma((CHUNKS, 2)),
            dma((CHUNKS, 2)),
            dma((CHUNKS, 2)),
            dma((CHUNKS, 2)),
            dma((CHUNKS, 2)),
            dma((CHUNKS, 2)),
            dma((2,)),
            dma((2,)),
            dma((LEVELS, 2)),
            dma((LEVELS, 2)),
            dma((LEVELS, 2)),
            dma((LEVELS, 2)),
            dma((2,)),
            dma((2,)),
        ],
        compiler_params=pltpu.CompilerParams(
            collective_id=0, has_side_effects=True, vmem_limit_bytes=60 * 1024 * 1024
        ),
    )(near_mask, points, weights, leaf_skeleton, node_skeleton)
    out = [jax.ShapeDtypeStruct((rows, rhs), bf16), jax.ShapeDtypeStruct((rows, rhs), jnp.float32)]
    every = pl.BlockSpec(memory_space=vmem)
    return pl.pallas_call(
        finish,
        out_shape=out,
        in_specs=[every] * 3,
        out_specs=[hbm] * 2,
        scratch_shapes=[
            vmem((rows, rhs), bf16),
            vmem((rows, rhs), jnp.float32),
            dma((2, BLOCKS)),
        ],
        compiler_params=pltpu.CompilerParams(vmem_limit_bytes=16 * 1024 * 1024),
    )(total, weights, targets)


def solution(mesh):
    placed = (
        P("leaf", None),
        P("leaf", None),
        P("leaf", None),
        P("leaf", None),
        P("leaf", None),
        P(None, "leaf", None),
    )
    return jax.shard_map(
        functools.partial(local, mesh.shape["leaf"]),
        mesh=mesh,
        in_specs=placed,
        out_specs=(P("leaf", None), P("leaf", None)),
        check_vma=False,
    )
```
